32 devices in a mesh: grp: 2 (over y), ctx: 4 (over z), head: 4 (over x, core).
Axes of the slice: x: 2, y: 2, z: 4, core: 2. Of those that a mesh axis runs over, the one named last changes fastest.
Arguments:
- inputs: bfloat16 [8192, 2560], P(('grp', 'ctx'), 'head'), parts along dimension 0, may hold values from -0.29882812 to 0.29882812
- write_coeffs: bfloat16 [8192, 128], P(('grp', 'ctx')), parts along dimension 0, may hold values from -1.796875 to 1.796875
- read_coeffs: bfloat16 [8192, 128], P(('grp', 'ctx')), parts along dimension 0, may hold values from -1.796875 to 1.796875
- log_decay: float32 [8192, 40], P(('grp', 'ctx'), 'head'), parts along dimension 0, may hold values from -1.6 to 0
- out_grad: bfloat16 [8192, 2560], P(('grp', 'ctx'), 'head'), parts along dimension 0, may hold values from -0.29882812 to 0.29882812
Outputs:
- outputs: bfloat16 [8192, 2560], P(('grp', 'ctx'), 'head'), parts along dimension 0
- in_grad: bfloat16 [8192, 2560], P(('grp', 'ctx'), 'head'), parts along dimension 0
- write_grad: float32 [8192, 128], P(('grp', 'ctx')), parts along dimension 0
- read_grad: float32 [8192, 128], P(('grp', 'ctx')), parts along dimension 0
- decay_grad: float32 [8192, 40], P(('grp', 'ctx'), 'head'), parts along dimension 0
The draws below stay inside these ranges and needn't reach their ends.
There are 2 independent parts, one for each index of `grp`. The reference program is written for one: setup_inputs(seed, part) draws one part's arguments, and reference() takes and returns one part's arrays. A program takes and returns all parts, laid end to end along the dimension named above; each array names one. Nothing has to cross between parts.
All inputs are finite; a program needn't handle non-finite values.
Results may differ from the reference program's by a relative error of at most 0.0071.
Values sent between devices are 32-bit elements; how exact they have to be, the bound alone decides.
A program may use at most 64 MiB of HBM per device.

```python
import jax
import jax.numpy as jnp
from jax import lax

MIXER_HEADS = 40
HEAD_DIM = 64
STATE = 128
BLOCK = 256
TOK_DEV = 1024
SEQUENCE_LENGTH = 4096


def draw_log_decay(key, part):
    random_subkeys = jax.random.split(jax.random.fold_in(key, 11), 7)
    fast_share = 0.5
    is_quick = jax.random.bernoulli(random_subkeys[0], fast_share, (MIXER_HEADS,))
    quick_rate = jax.random.uniform(random_subkeys[1], (MIXER_HEADS,), jnp.float32, 1.0 / 50.0, 1.0 / 30.0)
    slow_rate = jax.random.uniform(random_subkeys[2], (MIXER_HEADS,), jnp.float32, 0.2, 0.5) / SEQUENCE_LENGTH
    step_rates = jnp.where(is_quick, quick_rate, slow_rate)
    roughness = jax.random.uniform(random_subkeys[3], (SEQUENCE_LENGTH // TOK_DEV, TOK_DEV, MIXER_HEADS), jnp.float32, 0.5, 1.5)
    device_factor = jax.random.uniform(random_subkeys[4], (SEQUENCE_LENGTH // TOK_DEV, 1, MIXER_HEADS), jnp.float32, 0.7, 1.4)
    stable_baseline = (roughness * device_factor).reshape(SEQUENCE_LENGTH, MIXER_HEADS) * step_rates[None, :]
    spike_locations = jax.random.randint(random_subkeys[5], (3,), 0, SEQUENCE_LENGTH)
    spike_penalty = jax.random.uniform(random_subkeys[6], (3, MIXER_HEADS), jnp.float32, 0.22, 0.5)
    spike_matches = (jnp.arange(SEQUENCE_LENGTH)[:, None] == spike_locations[None, :]).astype(jnp.float32)
    spike_events = jnp.sum(spike_matches[:, :, None] * spike_penalty[None, :, :], axis=1)
    return -(stable_baseline + spike_events)


def steps_of(stream_key, dims, shards, smallest, high):
    def one(axis_at, shards_of):
        draws = jax.random.uniform(jax.random.fold_in(jax.random.fold_in(stream_key, 6), axis_at), (shards_of,), jnp.float32, smallest / len(shards), high / len(shards))
        return jnp.repeat(jnp.exp(draws), dims[axis_at] // shards_of).reshape((-1,) + (1,) * (len(dims) - axis_at - 1))

    loudness = one(*shards[0])
    for cut in shards[1:]:
        loudness = loudness * one(*cut)
    return loudness


def bell_draw(own_key, shape, deviation, limit, shards=(), held_as=jnp.bfloat16):
    result = jax.random.normal(own_key, shape, jnp.float32) * deviation
    if len(shards) > 0:
        result = steps_of(own_key, shape, shards, -0.22, 0.18) * result
    return jnp.clip(result, min=-limit, max=limit).astype(held_as)


def setup_inputs(seed: int = 0, part: int = 0) -> dict:
    key_list = jax.random.split(jax.random.key(seed), 6)
    own_keys = jax.random.split(jax.random.fold_in(key_list[5], part), 6)
    inputs = bell_draw(own_keys[0], (SEQUENCE_LENGTH, MIXER_HEADS * HEAD_DIM), 0.05, 0.29882812, ((0, 4), (1, 4)))
    write_coeffs = bell_draw(own_keys[1], (SEQUENCE_LENGTH, STATE), 0.3, 1.796875, ((0, 4),))
    read_coeffs = bell_draw(own_keys[2], (SEQUENCE_LENGTH, STATE), 0.3, 1.796875, ((0, 4),))
    log_decay = draw_log_decay(jax.random.fold_in(jax.random.fold_in(key_list[5], part), 71), part)
    out_grad = bell_draw(own_keys[4], (SEQUENCE_LENGTH, MIXER_HEADS * HEAD_DIM), 0.05, 0.29882812, ((0, 4), (1, 4)))
    return dict(inputs=inputs, write_coeffs=write_coeffs, read_coeffs=read_coeffs, log_decay=log_decay, out_grad=out_grad)


def rounded(values):
    return lax.optimization_barrier(values.astype(jnp.bfloat16)).astype(jnp.float32)


def split_blocks(array):
    return array.reshape((SEQUENCE_LENGTH // BLOCK, BLOCK) + array.shape[1:])


def product(form, left, right):
    return jnp.einsum(form, left, right, precision=lax.Precision.HIGHEST)


def inner_terms(pieces):
    inputs, write_c, read_c, running, grads = pieces
    totals = running[-1:, :]
    across = running.T
    spread = across[:, :, None] - across[:, None, :]
    causal = jnp.arange(BLOCK)[:, None] >= jnp.arange(BLOCK)[None, :]
    decays = jnp.where(causal, jnp.exp(jnp.where(causal, spread, 0.0)), 0.0)
    scores = jnp.dot(read_c, write_c.T, preferred_element_type=jnp.float32)
    weights = rounded(scores[None] * decays)
    x_wide = inputs.astype(jnp.float32)
    dy_wide = grads.astype(jnp.float32)
    b_wide = write_c.astype(jnp.float32)
    c_wide = read_c.astype(jnp.float32)
    y_inner = product("hts,shp->thp", weights, x_wide)
    dx_inner = product("hts,thp->shp", weights, dy_wide)
    pairs = product("thp,shp->hts", dy_wide, x_wide)
    pair_weights = rounded(pairs * decays)
    dc_inner = product("hts,sn->tn", pair_weights, b_wide)
    db_inner = product("hts,tn->sn", pair_weights, c_wide)
    grow = jnp.exp(running)[:, :, None]
    shrink = jnp.exp(totals - running)[:, :, None]
    block_state = product("sn,shp->hnp", b_wide, rounded(x_wide * shrink))
    block_adjoint = product("tn,thp->hnp", c_wide, rounded(dy_wide * grow))
    return y_inner, dx_inner, dc_inner, db_inner, block_state, block_adjoint, jnp.exp(totals[0])


def outer_terms(pieces):
    inputs, write_c, read_c, running, grads, state, adjoint = pieces
    totals = running[-1:, :]
    grow = jnp.exp(running)[:, :, None]
    shrink = jnp.exp(totals - running)[:, :, None]
    x_wide = inputs.astype(jnp.float32)
    dy_wide = grads.astype(jnp.float32)
    y_outer = grow * product("tn,hnp->thp", read_c.astype(jnp.float32), state)
    dx_outer = shrink * product("sn,hnp->shp", write_c.astype(jnp.float32), adjoint)
    dc_outer = product("thp,hnp->tn", dy_wide * grow, state)
    db_outer = product("shp,hnp->sn", x_wide * shrink, adjoint)
    return y_outer, dx_outer, dc_outer, db_outer


def reference(inputs, write_coeffs, read_coeffs, log_decay, out_grad):
    x_blocks = split_blocks(inputs.reshape(SEQUENCE_LENGTH, MIXER_HEADS, HEAD_DIM))
    dy_blocks = split_blocks(out_grad.reshape(SEQUENCE_LENGTH, MIXER_HEADS, HEAD_DIM))
    b_blocks = split_blocks(write_coeffs)
    c_blocks = split_blocks(read_coeffs)
    running = jnp.cumsum(split_blocks(log_decay), axis=1)
    y_inner, dx_inner, dc_inner, db_inner, states, adjoints, gains = lax.map(
        inner_terms, (x_blocks, b_blocks, c_blocks, running, dy_blocks))
    empty = jnp.zeros((MIXER_HEADS, STATE, HEAD_DIM), jnp.float32)

    def advance(carry, item):
        gain, piece = item
        return gain[:, None, None] * carry + piece, carry

    _, entering = lax.scan(advance, empty, (gains, states))
    _, leaving = lax.scan(advance, empty, (gains, adjoints), reverse=True)
    y_outer, dx_outer, dc_outer, db_outer = lax.map(
        outer_terms, (x_blocks, b_blocks, c_blocks, running, dy_blocks, entering, leaving))
    y_full = y_inner + y_outer
    dx_full = dx_inner + dx_outer
    read_grad = (dc_inner + dc_outer).reshape(SEQUENCE_LENGTH, STATE)
    write_grad = (db_inner + db_outer).reshape(SEQUENCE_LENGTH, STATE)
    balance = jnp.sum(dy_blocks.astype(jnp.float32) * y_full, axis=-1) - jnp.sum(x_blocks.astype(jnp.float32) * dx_full, axis=-1)
    balance = balance.reshape(SEQUENCE_LENGTH, MIXER_HEADS)
    decay_grad = jnp.flip(jnp.cumsum(jnp.flip(balance, 0), axis=0), 0)
    outputs = y_full.reshape(SEQUENCE_LENGTH, MIXER_HEADS * HEAD_DIM).astype(jnp.bfloat16)
    in_grad = dx_full.reshape(SEQUENCE_LENGTH, MIXER_HEADS * HEAD_DIM).astype(jnp.bfloat16)
    return outputs, in_grad, write_grad, read_grad, decay_grad
```

```python
import functools
import math

import jax
import jax.numpy as jnp
from jax import lax
from jax.experimental import pallas as pl
from jax.experimental.pallas import tpu as pltpu
from jax.sharding import PartitionSpec as P

HEAD_DIM = 64
STATE = 128
BLOCK = 256
LANES = 128
HOP_UNITS = 7
CHUNK_UNITS = 3
LOG2E = math.log2(math.e)
F32 = jnp.float32
BF16 = jnp.bfloat16
MESH = pl.DeviceIdType.MESH


def mxu(left, right, contract, precision=None):
    return lax.dot_general(
        left, right, (contract, ((), ())), preferred_element_type=F32, precision=precision
    )


def exact(left, right, contract=((1,), (0,))):
    return mxu(left, right, contract, lax.Precision.HIGHEST)


def iota(shape, dim):
    return lax.broadcasted_iota(jnp.int32, shape, dim)


def mixer_kernel(
    ring, chips, heads, blocks,
    x_hbm, b_hbm, c_hbm, ld_ref, dy_hbm,
    y_hbm, dx_hbm, db_hbm, dc_hbm, dg_ref,
    vec, coef, ldp, runc, runr, scale, gain, scaled, pieces, states, dev, inc, out_state,
    inner, rounded_out, grads, ptotal, bal, mate_in, far_in, back_in,
    load_sem, store_sem, grad_store_sem,
    chain_send, chain_recv, mate_send, mate_recv, far_send, far_recv, back_send, back_recv,
):
    place = lax.axis_index("ctx")
    head = lax.axis_index("head")
    core = lax.rem(head, 2)
    mate = head + 1 - 2 * core
    chip = lax.div(head, 2)
    pairs = heads // 2
    width = heads * HEAD_DIM
    half = BLOCK // 2

    loads = [
        pltpu.make_async_copy(dy_hbm, vec.at[0], load_sem.at[0]),
        pltpu.make_async_copy(x_hbm, vec.at[1], load_sem.at[1]),
        pltpu.make_async_copy(c_hbm, coef.at[0], load_sem.at[2]),
        pltpu.make_async_copy(b_hbm, coef.at[1], load_sem.at[3]),
    ]
    for copy in loads:
        copy.start()

    barrier = pltpu.get_barrier_semaphore()
    pl.semaphore_signal(barrier, inc=1, device_id={"head": mate}, device_id_type=MESH)
    for hop in range(1, chips):
        pl.semaphore_signal(
            barrier, inc=1, device_id={"head": lax.rem(head + 2 * hop, 2 * chips)}, device_id_type=MESH
        )

    @pl.when(place > 0)
    def _():
        pl.semaphore_signal(barrier, inc=1, device_id={"ctx": place - 1}, device_id_type=MESH)

    @pl.when(place < ring - 1)
    def _():
        pl.semaphore_signal(barrier, inc=1, device_id={"ctx": place + 1}, device_id_type=MESH)

    ldp[...] = jnp.zeros_like(ldp)
    ldp[:, 0:heads] = ld_ref[...]
    lower = (iota((BLOCK, BLOCK), 0) >= iota((BLOCK, BLOCK), 1)).astype(F32)
    spread = (iota((LANES, width), 0) == lax.div(iota((LANES, width), 1), HEAD_DIM)).astype(F32)

    @pl.loop(0, blocks)
    def _(j):
        rows = pl.ds(pl.multiple_of(j * BLOCK, BLOCK), BLOCK)
        run = exact(lower, ldp[rows, :]) * LOG2E
        runc[j] = run
        runr[j] = run.T
        wide = exact(run, spread)
        total = wide[BLOCK - 1 :, :]
        scale[0, rows, :] = jnp.exp2(wide)
        scale[1, rows, :] = jnp.exp2(total - wide)
        gain[j] = jnp.broadcast_to(jnp.exp2(total), (8, width))

    for copy in loads:
        copy.wait()

    @pl.loop(0, 2 * blocks)
    def _(i):
        d = i // blocks
        j = i % blocks
        rows = pl.ds(pl.multiple_of(j * BLOCK, BLOCK), BLOCK)
        row = (vec[d, rows, :].astype(F32) * scale[d, rows, :]).astype(BF16)
        scaled[d, rows, :] = row
        pieces[1 - d, j] = mxu(coef[d, rows, :], row, ((0,), (0,)))

    product = gain[0, 0:1, :]
    for j in range(1, blocks):
        product = product * gain[j, 0:1, :]
    forward = pieces[0, 0]
    backward = pieces[1, blocks - 1]
    for j in range(1, blocks):
        forward = gain[j, 0:1, :] * forward + pieces[0, j]
        k = blocks - 1 - j
        backward = gain[k, 0:1, :] * backward + pieces[1, k]
    for p in range(pairs):
        lanes = slice(p * LANES, (p + 1) * LANES)
        dev[0, p] = forward[:, lanes]
        dev[1, p] = backward[:, lanes]
        gain[blocks + p, :, 0:LANES] = jnp.broadcast_to(product[:, lanes], (8, LANES))

    pl.semaphore_wait(barrier, chips + (place > 0).astype(jnp.int32) + (place < ring - 1).astype(jnp.int32))

    first = (2 * place > ring - 1).astype(jnp.int32)
    second = 1 - first

    def hops(d):
        return jnp.where(d == 0, place, ring - 1 - place)

    def chain_copy(d, p):
        target = jnp.where(d == 0, place + 1, place - 1)
        return pltpu.make_async_remote_copy(
            src_ref=out_state.at[d, p],
            dst_ref=inc.at[d, p],
            send_sem=chain_send.at[d, p],
            recv_sem=chain_recv.at[d, p],
            device_id={"ctx": jnp.clip(target, 0, ring - 1)},
            device_id_type=MESH,
        )

    def relay(d, p):
        chain_copy(d, p).wait_recv()

        @pl.when(hops(d) < ring - 1)
        def _():
            out_state[d, p] = gain[blocks + p, 0:1, 0:LANES] * inc[d, p] + dev[d, p]
            chain_copy(d, p).start()

    for d in range(2):

        @pl.when(hops(d) == 0)
        def _():
            @pl.loop(0, pairs)
            def _(p):
                inc[d, p] = jnp.zeros((STATE, LANES), F32)
                if ring > 1:
                    out_state[d, p] = dev[d, p]
                    chain_copy(d, p).start()

    def tick(unit):
        for d in (first, second):
            since = unit - HOP_UNITS * hops(d)
            p = jnp.maximum(since, 0) // CHUNK_UNITS

            @pl.when((hops(d) > 0) & (since >= 0) & (since == p * CHUNK_UNITS) & (p < pairs))
            def _():
                relay(d, p)

    last_unit = HOP_UNITS * (ring - 1) + CHUNK_UNITS * (pairs - 1) + 1

    low_lanes = iota((1, LANES), 1) < HEAD_DIM

    @pl.loop(0, blocks)
    def _(j):
        rows = pl.ds(pl.multiple_of(j * BLOCK, BLOCK), BLOCK)
        causal = iota((BLOCK, BLOCK), 0) >= iota((BLOCK, BLOCK), 1)
        scores = jnp.where(causal, mxu(coef[0, rows, :], coef[1, rows, :], ((1,), (1,))), 0.0)
        ptotal[0] = scores
        for p in range(pairs):
            lanes = slice(p * LANES, (p + 1) * LANES)
            x2 = vec[1, rows, lanes]
            dy2 = vec[0, rows, lanes]
            y2 = None
            for k in range(2):
                h = 2 * p + k
                mine = low_lanes if k == 0 else jnp.logical_not(low_lanes)
                xm = jnp.where(mine, x2, jnp.zeros_like(x2))
                dym = jnp.where(mine, dy2, jnp.zeros_like(dy2))
                decays = jnp.exp2(jnp.minimum(runc[j, :, h : h + 1] - runr[j, h : h + 1, :], 0.0))
                weights = (ptotal[0] * decays).astype(BF16)
                pair = mxu(dy2, xm, ((1,), (1,))) * decays
                if h == 0:
                    ptotal[1] = pair
                else:
                    ptotal[1] += pair
                y_add = mxu(weights, xm, ((1,), (0,)))
                dx_add = mxu(weights, dym, ((0,), (0,)))
                y2 = y_add if y2 is None else y2 + y_add
                dx2 = dx_add if k == 0 else dx2 + dx_add
            inner[0, rows, lanes] = y2
            inner[1, rows, lanes] = dx2
            tick(j * pairs + p)
        both = jnp.where(causal, ptotal[1], 0.0).astype(BF16)
        grads[0, rows, :] = mxu(both, coef[1, rows, :], ((1,), (0,)))
        grads[1, rows, :] = mxu(both, coef[0, rows, :], ((0,), (0,)))

    own_rows = core * half
    mate_rows = half - own_rows

    def piece_of(j, at):
        return pl.ds(pl.multiple_of(j * BLOCK + at, half), half)

    def mate_copy(d, j):
        return pltpu.make_async_remote_copy(
            src_ref=grads.at[d, piece_of(j, mate_rows), :],
            dst_ref=mate_in.at[d, j],
            send_sem=mate_send.at[d, j],
            recv_sem=mate_recv.at[d, j],
            device_id={"head": mate},
            device_id_type=MESH,
        )

    def far_copy(d, j, hop):
        return pltpu.make_async_remote_copy(
            src_ref=mate_in.at[d, j],
            dst_ref=far_in.at[d, j, chip],
            send_sem=far_send.at[d, j, hop],
            recv_sem=far_recv.at[d, j, chip],
            device_id={"head": lax.rem(head + 2 * hop, 2 * chips)},
            device_id_type=MESH,
        )

    def far_arrival(d, j, hop):
        source = lax.rem(chip + chips - hop, chips)
        return pltpu.make_async_remote_copy(
            src_ref=mate_in.at[d, j],
            dst_ref=far_in.at[d, j, source],
            send_sem=far_send.at[d, j, hop],
            recv_sem=far_recv.at[d, j, source],
            device_id={"head": lax.rem(head + 2 * hop, 2 * chips)},
            device_id_type=MESH,
        )

    def back_copy(d, j):
        return pltpu.make_async_remote_copy(
            src_ref=grads.at[d, piece_of(j, own_rows), :],
            dst_ref=back_in.at[d, j],
            send_sem=back_send.at[d, j],
            recv_sem=back_recv.at[d, j],
            device_id={"head": mate},
            device_id_type=MESH,
        )

    def local_sum(d, j):
        mate_copy(d, j).wait_recv()
        total = mate_in[d, j] + grads[d, piece_of(j, own_rows), :]
        mate_in[d, j] = total
        far_in[d, j, chip] = total
        for hop in range(1, chips):
            far_copy(d, j, hop).start()

    def far_sum(d, j):
        for hop in range(1, chips):
            far_arrival(d, j, hop).wait_recv()
        total = far_in[d, j, 0]
        for source in range(1, chips):
            total = total + far_in[d, j, source]
        grads[d, piece_of(j, own_rows), :] = total
        back_copy(d, j).start()

    def order(d, i):
        return jnp.where(d == 0, i, blocks - 1 - i)

    def outer(d, start, is_second):
        state = jnp.concatenate([inc[d, p] for p in range(pairs)], axis=1)
        states[d, blocks] = state

        @pl.loop(0, blocks)
        def _(i):
            j = order(d, i)
            rows = pl.ds(pl.multiple_of(j * BLOCK, BLOCK), BLOCK)
            now = states[d, blocks]
            states[d, j] = now
            states[d, blocks] = gain[j, 0:1, :] * now + pieces[d, j]
            held = now.astype(BF16)
            grads[d, rows, :] += mxu(scaled[d, rows, :], held, ((1,), (1,)))
            mate_copy(d, j).start()
            full = inner[d, rows, :] + scale[d, rows, :] * mxu(coef[d, rows, :], held, ((1,), (0,)))
            rounded_out[d, rows, :] = full.astype(BF16)
            term = vec[d, rows, :].astype(F32) * full
            high = term.astype(BF16)
            low = (term - high.astype(F32)).astype(BF16)
            gather = spread.astype(BF16)
            summed = mxu(high, gather, ((1,), (1,))) + mxu(low, gather, ((1,), (1,)))
            summed = jnp.where(d == 0, summed, -summed)
            if is_second:
                bal[rows, :] += summed
            else:
                bal[rows, :] = summed
                tick(start + i)

            @pl.when(i > 0)
            def _():
                local_sum(d, order(d, i - 1))

        local_sum(d, order(d, blocks - 1))

        @pl.when(d == 0)
        def _():
            pltpu.make_async_copy(rounded_out.at[0], y_hbm, store_sem.at[0]).start()

        @pl.when(d == 1)
        def _():
            pltpu.make_async_copy(rounded_out.at[1], dx_hbm, store_sem.at[1]).start()

    units = blocks * pairs

    @pl.loop(units, jnp.maximum(units, HOP_UNITS * hops(first) + CHUNK_UNITS * (pairs - 1) + 1))
    def _(u):
        tick(u)

    start = jnp.maximum(units, HOP_UNITS * hops(first) + CHUNK_UNITS * (pairs - 1) + 1)
    outer(first, start, False)

    @pl.loop(start + blocks, jnp.maximum(start + blocks, last_unit))
    def _(u):
        tick(u)

    @pl.loop(0, blocks)
    def _(i):
        far_sum(first, order(first, i))

    outer(second, 0, True)

    gather = spread

    @pl.loop(0, blocks)
    def _(j):
        rows = pl.ds(pl.multiple_of(j * BLOCK, BLOCK), BLOCK)
        joint = jnp.sum(states[0, j + 1] * states[1, j], axis=0, keepdims=True)
        later = exact(jnp.broadcast_to(joint, (8, width)), gather, ((1,), (1,)))[0:1, :]
        suffix = exact(lower, bal[rows, :], ((0,), (0,))) + later
        dg_ref[rows, :] = suffix[:, 0:heads]

    @pl.loop(0, blocks)
    def _(i):
        far_sum(second, order(second, i))

    def own_store(d, j):
        target = dc_hbm if d == 0 else db_hbm
        rows = piece_of(j, own_rows)
        return pltpu.make_async_copy(grads.at[d, rows, :], target.at[rows, :], grad_store_sem.at[d, j, 0])

    def mate_store(d, j):
        target = dc_hbm if d == 0 else db_hbm
        rows = piece_of(j, mate_rows)
        return pltpu.make_async_copy(back_in.at[d, j], target.at[rows, :], grad_store_sem.at[d, j, 1])

    @pl.loop(0, blocks)
    def _(j):
        for d in range(2):
            own_store(d, j).start()

    @pl.loop(0, blocks)
    def _(j):
        for d in range(2):
            back_copy(d, j).wait_recv()
            mate_store(d, j).start()

    @pl.loop(0, blocks)
    def _(j):
        for d in range(2):
            own_store(d, j).wait()
            mate_store(d, j).wait()
            mate_copy(d, j).wait_send()
            back_copy(d, j).wait_send()
            for hop in range(1, chips):
                far_copy(d, j, hop).wait_send()

    pltpu.make_async_copy(rounded_out.at[0], y_hbm, store_sem.at[0]).wait()
    pltpu.make_async_copy(rounded_out.at[1], dx_hbm, store_sem.at[1]).wait()

    for d in range(2):

        @pl.when(hops(d) < ring - 1)
        def _():
            @pl.loop(0, pairs)
            def _(p):
                chain_copy(d, p).wait_send()


def per_device(ring, chips, inputs, write_coeffs, read_coeffs, log_decay, out_grad):
    tokens = inputs.shape[0]
    real = log_decay.shape[1]
    heads = real + real % 2
    if heads > real:
        extra = ((0, 0), (0, (heads - real) * HEAD_DIM))
        inputs = jnp.pad(inputs, extra)
        out_grad = jnp.pad(out_grad, extra)
        log_decay = jnp.pad(log_decay, ((0, 0), (0, heads - real)))
    width = heads * HEAD_DIM
    blocks = tokens // BLOCK
    pairs = heads // 2
    half = BLOCK // 2
    any_spec = pl.BlockSpec(memory_space=pl.ANY)
    vmem_spec = pl.BlockSpec(memory_space=pltpu.VMEM)
    dma = pltpu.SemaphoreType.DMA
    y, dx, db, dc, dg = pl.pallas_call(
        functools.partial(mixer_kernel, ring, chips, heads, blocks),
        out_shape=(
            jax.ShapeDtypeStruct((tokens, width), BF16),
            jax.ShapeDtypeStruct((tokens, width), BF16),
            jax.ShapeDtypeStruct((tokens, STATE), F32),
            jax.ShapeDtypeStruct((tokens, STATE), F32),
            jax.ShapeDtypeStruct((tokens, heads), F32),
        ),
        in_specs=[any_spec, any_spec, any_spec, vmem_spec, any_spec],
        out_specs=(any_spec, any_spec, any_spec, any_spec, vmem_spec),
        scratch_shapes=[
            pltpu.VMEM((2, tokens, width), BF16),
            pltpu.VMEM((2, tokens, STATE), BF16),
            pltpu.VMEM((tokens, LANES), F32),
            pltpu.VMEM((blocks, BLOCK, LANES), F32),
            pltpu.VMEM((blocks, LANES, BLOCK), F32),
            pltpu.VMEM((2, tokens, width), F32),
            pltpu.VMEM((blocks + pairs, 8, width), F32),
            pltpu.VMEM((2, tokens, width), BF16),
            pltpu.VMEM((2, blocks, STATE, width), F32),
            pltpu.VMEM((2, blocks + 1, STATE, width), F32),
            pltpu.VMEM((2, pairs, STATE, LANES), F32),
            pltpu.VMEM((2, pairs, STATE, LANES), F32),
            pltpu.VMEM((2, pairs, STATE, LANES), F32),
            pltpu.VMEM((2, tokens, width), F32),
            pltpu.VMEM((2, tokens, width), BF16),
            pltpu.VMEM((2, tokens, STATE), F32),
            pltpu.VMEM((2, BLOCK, BLOCK), F32),
            pltpu.VMEM((tokens, LANES), F32),
            pltpu.VMEM((2, blocks, half, STATE), F32),
            pltpu.VMEM((2, blocks, chips, half, STATE), F32),
            pltpu.VMEM((2, blocks, half, STATE), F32),
            dma((4,)),
            dma((2,)),
            dma((2, blocks, 2)),
            dma((2, pairs)),
            dma((2, pairs)),
            dma((2, blocks)),
            dma((2, blocks)),
            dma((2, blocks, chips)),
            dma((2, blocks, chips)),
            dma((2, blocks)),
            dma((2, blocks)),
        ],
        compiler_params=pltpu.CompilerParams(
            collective_id=0, has_side_effects=True, vmem_limit_bytes=56 * 1024 * 1024
        ),
    )(inputs, write_coeffs, read_coeffs, log_decay, out_grad)
    if heads > real:
        y = y[:, : real * HEAD_DIM]
        dx = dx[:, : real * HEAD_DIM]
        dg = dg[:, :real]
    return (y, dx, db, dc, dg)


def solution(mesh):
    in_specs = (
        P(("grp", "ctx"), "head"),
        P(("grp", "ctx"), None),
        P(("grp", "ctx"), None),
        P(("grp", "ctx"), "head"),
        P(("grp", "ctx"), "head"),
    )
    out_specs = (
        P(("grp", "ctx"), "head"),
        P(("grp", "ctx"), "head"),
        P(("grp", "ctx"), None),
        P(("grp", "ctx"), None),
        P(("grp", "ctx"), "head"),
    )
    return jax.shard_map(
        functools.partial(per_device, mesh.shape["ctx"], mesh.shape["head"] // 2),
        mesh=mesh,
        in_specs=in_specs,
        out_specs=out_specs,
        check_vma=False,
    )
```

```python
import functools
import math

import jax
import jax.numpy as jnp
from jax import lax
from jax.experimental import pallas as pl
from jax.experimental.pallas import tpu as pltpu
from jax.sharding import PartitionSpec as P

HEAD_DIM = 64
STATE = 128
BLOCK = 256
LANES = 128
HOP_UNITS = 7
CHUNK_UNITS = 3
LOG2E = math.log2(math.e)
F32 = jnp.float32
BF16 = jnp.bfloat16
MESH = pl.DeviceIdType.MESH


def mxu(left, right, contract, precision=None):
    return lax.dot_general(
        left, right, (contract, ((), ())), preferred_element_type=F32, precision=precision
    )


def thirds(values):
    high = values.astype(BF16)
    rest = values - high.astype(F32)
    middle = rest.astype(BF16)
    low = (rest - middle.astype(F32)).astype(BF16)
    return jnp.concatenate([high, middle, low], axis=0)


def iota(shape, dim):
    return lax.broadcasted_iota(jnp.int32, shape, dim)


def mixer_kernel(
    ring, chips, heads, blocks,
    x_hbm, b_hbm, c_hbm, ld_ref, dy_hbm,
    y_hbm, dx_hbm, db_hbm, dc_hbm, dg_ref,
    vec, coef, ldp, runc, runr, scale, gain, scaled, pieces, states, states_held, dev, inc, out_state,
    inner, rounded_out, grads, ptotal, bal, mate_in, far_in, back_in,
    load_sem, store_sem, grad_store_sem,
    chain_send, chain_recv, mate_send, mate_recv, far_send, far_recv, back_send, back_recv,
):
    place = lax.axis_index("ctx")
    head = lax.axis_index("head")
    core = lax.rem(head, 2)
    mate = head + 1 - 2 * core
    chip = lax.div(head, 2)
    pairs = heads // 2
    width = heads * HEAD_DIM
    half = BLOCK // 2

    loads = [
        pltpu.make_async_copy(dy_hbm, vec.at[0], load_sem.at[0]),
        pltpu.make_async_copy(x_hbm, vec.at[1], load_sem.at[1]),
        pltpu.make_async_copy(c_hbm, coef.at[0], load_sem.at[2]),
        pltpu.make_async_copy(b_hbm, coef.at[1], load_sem.at[3]),
    ]
    for copy in loads:
        copy.start()

    barrier = pltpu.get_barrier_semaphore()
    pl.semaphore_signal(barrier, inc=1, device_id={"head": mate}, device_id_type=MESH)
    for hop in range(1, chips):
        pl.semaphore_signal(
            barrier, inc=1, device_id={"head": lax.rem(head + 2 * hop, 2 * chips)}, device_id_type=MESH
        )

    @pl.when(place > 0)
    def _():
        pl.semaphore_signal(barrier, inc=1, device_id={"ctx": place - 1}, device_id_type=MESH)

    @pl.when(place < ring - 1)
    def _():
        pl.semaphore_signal(barrier, inc=1, device_id={"ctx": place + 1}, device_id_type=MESH)

    slots = ldp.shape[0]
    ldp[...] = jnp.zeros_like(ldp)
    ldp[0:heads, :] = ld_ref[...]
    upper = (iota((BLOCK, BLOCK), 0) <= iota((BLOCK, BLOCK), 1)).astype(F32).astype(BF16)
    spread = (iota((slots, width), 0) == lax.div(iota((slots, width), 1), HEAD_DIM)).astype(F32)
    spread3 = jnp.concatenate([spread] * 3, axis=0).astype(BF16)
    gather = spread.astype(BF16)

    def joined(left3, right):
        three = mxu(left3, right, ((1,), (0,)))
        return three[0:slots] + three[slots : 2 * slots] + three[2 * slots :]

    for j in range(blocks):
        rows = slice(j * BLOCK, (j + 1) * BLOCK)
        run = joined(thirds(ldp[:, rows]), upper) * LOG2E
        runr[j] = run
        runc[j] = jnp.concatenate([run, jnp.zeros((LANES - slots, BLOCK), F32)], axis=0).T
        grow = mxu(thirds(jnp.exp2(run)), spread3, ((0,), (0,)))
        scale[0, rows, :] = grow
        scale[1, rows, :] = mxu(
            thirds(jnp.exp2(run[:, BLOCK - 1 :] - run)), spread3, ((0,), (0,))
        )
        gain[j] = jnp.broadcast_to(grow[BLOCK - 1 :, :], (8, width))

    for copy in loads:
        copy.wait()

    for j in range(blocks):
        for d in range(2):
            rows = slice(j * BLOCK, (j + 1) * BLOCK)
            row = (vec[d, rows, :].astype(F32) * scale[d, rows, :]).astype(BF16)
            scaled[d, rows, :] = row
            pieces[1 - d, j] = mxu(coef[d, rows, :], row, ((0,), (0,)))

    for p in range(pairs):
        lanes = slice(p * LANES, (p + 1) * LANES)
        product = gain[0, 0:1, lanes]
        forward = pieces[0, 0, :, lanes]
        backward = pieces[1, blocks - 1, :, lanes]
        for j in range(1, blocks):
            product = product * gain[j, 0:1, lanes]
            forward = gain[j, 0:1, lanes] * forward + pieces[0, j, :, lanes]
            k = blocks - 1 - j
            backward = gain[k, 0:1, lanes] * backward + pieces[1, k, :, lanes]
        dev[0, p] = forward
        dev[1, p] = backward
        gain[blocks + p, :, 0:LANES] = jnp.broadcast_to(product, (8, LANES))

    pl.semaphore_wait(barrier, chips + (place > 0).astype(jnp.int32) + (place < ring - 1).astype(jnp.int32))

    first = (2 * place > ring - 1).astype(jnp.int32)
    second = 1 - first

    def hops(d):
        return jnp.where(d == 0, place, ring - 1 - place)

    def chain_copy(d, p):
        target = jnp.where(d == 0, place + 1, place - 1)
        return pltpu.make_async_remote_copy(
            src_ref=out_state.at[d, p],
            dst_ref=inc.at[d, p],
            send_sem=chain_send.at[d, p],
            recv_sem=chain_recv.at[d, p],
            device_id={"ctx": jnp.clip(target, 0, ring - 1)},
            device_id_type=MESH,
        )

    def relay(d, p):
        chain_copy(d, p).wait_recv()

        @pl.when(hops(d) < ring - 1)
        def _():
            out_state[d, p] = gain[blocks + p, 0:1, 0:LANES] * inc[d, p] + dev[d, p]
            chain_copy(d, p).start()

    for d in range(2):

        @pl.when(hops(d) == 0)
        def _():
            @pl.loop(0, pairs)
            def _(p):
                inc[d, p] = jnp.zeros((STATE, LANES), F32)
                if ring > 1:
                    out_state[d, p] = dev[d, p]
                    chain_copy(d, p).start()

    def tick(unit):
        for d in (first, second):
            since = unit - HOP_UNITS * hops(d)
            p = jnp.maximum(since, 0) // CHUNK_UNITS

            @pl.when((hops(d) > 0) & (since >= 0) & (since == p * CHUNK_UNITS) & (p < pairs))
            def _():
                relay(d, p)

    last_unit = HOP_UNITS * (ring - 1) + CHUNK_UNITS * (pairs - 1) + 1

    low_lanes = iota((1, LANES), 1) < HEAD_DIM

    @pl.loop(0, blocks)
    def _(j):
        rows = pl.ds(pl.multiple_of(j * BLOCK, BLOCK), BLOCK)
        causal = iota((BLOCK, BLOCK), 0) >= iota((BLOCK, BLOCK), 1)
        scores = jnp.where(causal, mxu(coef[0, rows, :], coef[1, rows, :], ((1,), (1,))), 0.0)
        ptotal[0] = scores
        for p in range(pairs):
            lanes = slice(p * LANES, (p + 1) * LANES)
            x2 = vec[1, rows, lanes]
            dy2 = vec[0, rows, lanes]
            y2 = None
            for k in range(2):
                h = 2 * p + k
                mine = low_lanes if k == 0 else jnp.logical_not(low_lanes)
                xm = jnp.where(mine, x2, jnp.zeros_like(x2))
                dym = jnp.where(mine, dy2, jnp.zeros_like(dy2))
                decays = jnp.exp2(jnp.minimum(runc[j, :, h : h + 1] - runr[j, h : h + 1, :], 0.0))
                weights = (ptotal[0] * decays).astype(BF16)
                pair = mxu(dy2, xm, ((1,), (1,))) * decays
                if h == 0:
                    ptotal[1] = pair
                else:
                    ptotal[1] += pair
                y_add = mxu(weights, xm, ((1,), (0,)))
                dx_add = mxu(weights, dym, ((0,), (0,)))
                y2 = y_add if y2 is None else y2 + y_add
                dx2 = dx_add if k == 0 else dx2 + dx_add
            inner[0, rows, lanes] = y2
            inner[1, rows, lanes] = dx2
            tick(j * pairs + p)
        both = jnp.where(causal, ptotal[1], 0.0).astype(BF16)
        grads[0, rows, :] = mxu(both, coef[1, rows, :], ((1,), (0,)))
        grads[1, rows, :] = mxu(both, coef[0, rows, :], ((0,), (0,)))

    own_rows = core * half
    mate_rows = half - own_rows

    def piece_of(j, at):
        return pl.ds(pl.multiple_of(j * BLOCK + at, half), half)

    def mate_copy(d, j):
        return pltpu.make_async_remote_copy(
            src_ref=grads.at[d, piece_of(j, mate_rows), :],
            dst_ref=mate_in.at[d, j],
            send_sem=mate_send.at[d, j],
            recv_sem=mate_recv.at[d, j],
            device_id={"head": mate},
            device_id_type=MESH,
        )

    def far_copy(d, j, hop):
        return pltpu.make_async_remote_copy(
            src_ref=mate_in.at[d, j],
            dst_ref=far_in.at[d, j, chip],
            send_sem=far_send.at[d, j, hop],
            recv_sem=far_recv.at[d, j, chip],
            device_id={"head": lax.rem(head + 2 * hop, 2 * chips)},
            device_id_type=MESH,
        )

    def far_arrival(d, j, hop):
        source = lax.rem(chip + chips - hop, chips)
        return pltpu.make_async_remote_copy(
            src_ref=mate_in.at[d, j],
            dst_ref=far_in.at[d, j, source],
            send_sem=far_send.at[d, j, hop],
            recv_sem=far_recv.at[d, j, source],
            device_id={"head": lax.rem(head + 2 * hop, 2 * chips)},
            device_id_type=MESH,
        )

    def back_copy(d, j):
        return pltpu.make_async_remote_copy(
            src_ref=grads.at[d, piece_of(j, own_rows), :],
            dst_ref=back_in.at[d, j],
            send_sem=back_send.at[d, j],
            recv_sem=back_recv.at[d, j],
            device_id={"head": mate},
            device_id_type=MESH,
        )

    def local_sum(d, j):
        mate_copy(d, j).wait_recv()
        total = mate_in[d, j] + grads[d, piece_of(j, own_rows), :]
        mate_in[d, j] = total
        far_in[d, j, chip] = total
        for hop in range(1, chips):
            far_copy(d, j, hop).start()

    def far_sum(d, j):
        for hop in range(1, chips):
            far_arrival(d, j, hop).wait_recv()
        total = far_in[d, j, 0]
        for source in range(1, chips):
            total = total + far_in[d, j, source]
        grads[d, piece_of(j, own_rows), :] = total
        back_copy(d, j).start()

    def order(d, i):
        return jnp.where(d == 0, i, blocks - 1 - i)

    def outer_grads(d, start, ticking):
        states[d, blocks] = jnp.concatenate([inc[d, p] for p in range(pairs)], axis=1)

        @pl.loop(0, blocks)
        def _(i):
            j = order(d, i)
            rows = pl.ds(pl.multiple_of(j * BLOCK, BLOCK), BLOCK)
            now = states[d, blocks]
            states[d, j] = now
            states[d, blocks] = gain[j, 0:1, :] * now + pieces[d, j]
            held = now.astype(BF16)
            states_held[d, j] = held
            grads[d, rows, :] += mxu(scaled[d, rows, :], held, ((1,), (1,)))
            mate_copy(d, j).start()
            if ticking:
                tick(start + i)

            @pl.when(i > 0)
            def _():
                local_sum(d, order(d, i - 1))

        local_sum(d, order(d, blocks - 1))

    def outer_rows(d, start, ticking):
        @pl.loop(0, blocks)
        def _(i):
            j = order(d, i)
            rows = pl.ds(pl.multiple_of(j * BLOCK, BLOCK), BLOCK)
            held = states_held[d, j]
            full = inner[d, rows, :] + scale[d, rows, :] * mxu(coef[d, rows, :], held, ((1,), (0,)))
            rounded_out[d, rows, :] = full.astype(BF16)
            term = vec[d, rows, :].astype(F32) * full
            high = term.astype(BF16)
            low = (term - high.astype(F32)).astype(BF16)
            summed = mxu(gather, high, ((1,), (1,))) + mxu(gather, low, ((1,), (1,)))
            summed = jnp.where(d == 0, summed, -summed)
            if ticking:
                bal[j] = summed
                tick(start + i)
            else:
                bal[j] += summed

        @pl.when(d == 0)
        def _():
            pltpu.make_async_copy(rounded_out.at[0], y_hbm, store_sem.at[0]).start()

        @pl.when(d == 1)
        def _():
            pltpu.make_async_copy(rounded_out.at[1], dx_hbm, store_sem.at[1]).start()

    units = blocks * pairs

    @pl.loop(units, jnp.maximum(units, HOP_UNITS * hops(first) + CHUNK_UNITS * (pairs - 1) + 1))
    def _(u):
        tick(u)

    start = jnp.maximum(units, HOP_UNITS * hops(first) + CHUNK_UNITS * (pairs - 1) + 1)
    outer_grads(first, start, True)
    outer_rows(first, start + blocks, True)
    start = start + 2 * blocks

    @pl.loop(start, jnp.maximum(start, last_unit))
    def _(u):
        tick(u)

    outer_grads(second, 0, False)

    @pl.loop(0, blocks)
    def _(i):
        far_sum(first, order(first, i))

    outer_rows(second, 0, False)

    for j in range(blocks):
        joint = jnp.sum(states[0, j + 1] * states[1, j], axis=0, keepdims=True)
        later = jnp.sum(spread * joint, axis=1, keepdims=True)
        lower = (iota((BLOCK, BLOCK), 0) >= iota((BLOCK, BLOCK), 1)).astype(F32).astype(BF16)
        suffix = joined(thirds(bal[j]), lower) + later
        dg_ref[:, j * BLOCK : (j + 1) * BLOCK] = suffix[0:heads, :]

    @pl.loop(0, blocks)
    def _(i):
        far_sum(second, order(second, i))

    def own_store(d, j):
        target = dc_hbm if d == 0 else db_hbm
        rows = piece_of(j, own_rows)
        return pltpu.make_async_copy(grads.at[d, rows, :], target.at[rows, :], grad_store_sem.at[d, j, 0])

    def mate_store(d, j):
        target = dc_hbm if d == 0 else db_hbm
        rows = piece_of(j, mate_rows)
        return pltpu.make_async_copy(back_in.at[d, j], target.at[rows, :], grad_store_sem.at[d, j, 1])

    @pl.loop(0, blocks)
    def _(j):
        for d in range(2):
            own_store(d, j).start()

    @pl.loop(0, blocks)
    def _(j):
        for d in range(2):
            back_copy(d, j).wait_recv()
            mate_store(d, j).start()

    @pl.loop(0, blocks)
    def _(j):
        for d in range(2):
            own_store(d, j).wait()
            mate_store(d, j).wait()
            mate_copy(d, j).wait_send()
            back_copy(d, j).wait_send()
            for hop in range(1, chips):
                far_copy(d, j, hop).wait_send()

    pltpu.make_async_copy(rounded_out.at[0], y_hbm, store_sem.at[0]).wait()
    pltpu.make_async_copy(rounded_out.at[1], dx_hbm, store_sem.at[1]).wait()

    for d in range(2):

        @pl.when(hops(d) < ring - 1)
        def _():
            @pl.loop(0, pairs)
            def _(p):
                chain_copy(d, p).wait_send()


def per_device(ring, chips, inputs, write_coeffs, read_coeffs, log_decay, out_grad):
    tokens = inputs.shape[0]
    real = log_decay.shape[1]
    heads = real + real % 2
    if heads > real:
        extra = ((0, 0), (0, (heads - real) * HEAD_DIM))
        inputs = jnp.pad(inputs, extra)
        out_grad = jnp.pad(out_grad, extra)
        log_decay = jnp.pad(log_decay, ((0, 0), (0, heads - real)))
    width = heads * HEAD_DIM
    blocks = tokens // BLOCK
    pairs = heads // 2
    half = BLOCK // 2
    slots = -(-heads // 16) * 16
    any_spec = pl.BlockSpec(memory_space=pl.ANY)
    vmem_spec = pl.BlockSpec(memory_space=pltpu.VMEM)
    dma = pltpu.SemaphoreType.DMA
    y, dx, db, dc, dg = pl.pallas_call(
        functools.partial(mixer_kernel, ring, chips, heads, blocks),
        out_shape=(
            jax.ShapeDtypeStruct((tokens, width), BF16),
            jax.ShapeDtypeStruct((tokens, width), BF16),
            jax.ShapeDtypeStruct((tokens, STATE), F32),
            jax.ShapeDtypeStruct((tokens, STATE), F32),
            jax.ShapeDtypeStruct((heads, tokens), F32),
        ),
        in_specs=[any_spec, any_spec, any_spec, vmem_spec, any_spec],
        out_specs=(any_spec, any_spec, any_spec, any_spec, vmem_spec),
        scratch_shapes=[
            pltpu.VMEM((2, tokens, width), BF16),
            pltpu.VMEM((2, tokens, STATE), BF16),
            pltpu.VMEM((slots, tokens), F32),
            pltpu.VMEM((blocks, BLOCK, LANES), F32),
            pltpu.VMEM((blocks, slots, BLOCK), F32),
            pltpu.VMEM((2, tokens, width), F32),
            pltpu.VMEM((blocks + pairs, 8, width), F32),
            pltpu.VMEM((2, tokens, width), BF16),
            pltpu.VMEM((2, blocks, STATE, width), F32),
            pltpu.VMEM((2, blocks + 1, STATE, width), F32),
            pltpu.VMEM((2, blocks, STATE, width), BF16),
            pltpu.VMEM((2, pairs, STATE, LANES), F32),
            pltpu.VMEM((2, pairs, STATE, LANES), F32),
            pltpu.VMEM((2, pairs, STATE, LANES), F32),
            pltpu.VMEM((2, tokens, width), F32),
            pltpu.VMEM((2, tokens, width), BF16),
            pltpu.VMEM((2, tokens, STATE), F32),
            pltpu.VMEM((2, BLOCK, BLOCK), F32),
            pltpu.VMEM((blocks, slots, BLOCK), F32),
            pltpu.VMEM((2, blocks, half, STATE), F32),
            pltpu.VMEM((2, blocks, chips, half, STATE), F32),
            pltpu.VMEM((2, blocks, half, STATE), F32),
            dma((4,)),
            dma((2,)),
            dma((2, blocks, 2)),
            dma((2, pairs)),
            dma((2, pairs)),
            dma((2, blocks)),
            dma((2, blocks)),
            dma((2, blocks, chips)),
            dma((2, blocks, chips)),
            dma((2, blocks)),
            dma((2, blocks)),
        ],
        compiler_params=pltpu.CompilerParams(
            collective_id=0, has_side_effects=True, vmem_limit_bytes=56 * 1024 * 1024
        ),
    )(inputs, write_coeffs, read_coeffs, log_decay.T, out_grad)
    dg = dg.T
    if heads > real:
        y = y[:, : real * HEAD_DIM]
        dx = dx[:, : real * HEAD_DIM]
        dg = dg[:, :real]
    return (y, dx, db, dc, dg)


def solution(mesh):
    in_specs = (
        P(("grp", "ctx"), "head"),
        P(("grp", "ctx"), None),
        P(("grp", "ctx"), None),
        P(("grp", "ctx"), "head"),
        P(("grp", "ctx"), "head"),
    )
    out_specs = (
        P(("grp", "ctx"), "head"),
        P(("grp", "ctx"), "head"),
        P(("grp", "ctx"), None),
        P(("grp", "ctx"), None),
        P(("grp", "ctx"), "head"),
    )
    return jax.shard_map(
        functools.partial(per_device, mesh.shape["ctx"], mesh.shape["head"] // 2),
        mesh=mesh,
        in_specs=in_specs,
        out_specs=out_specs,
        check_vma=False,
    )
```

```python
import functools
import math

import jax
import jax.numpy as jnp
from jax import lax
from jax.experimental import pallas as pl
from jax.experimental.pallas import tpu as pltpu
from jax.sharding import PartitionSpec as P

HEAD_DIM = 64
STATE = 128
BLOCK = 256
LANES = 128
HOP_UNITS = 7
CHUNK_UNITS = 3
LOG2E = math.log2(math.e)
F32 = jnp.float32
BF16 = jnp.bfloat16
MESH = pl.DeviceIdType.MESH


def mxu(left, right, contract, precision=None):
    return lax.dot_general(
        left, right, (contract, ((), ())), preferred_element_type=F32, precision=precision
    )


def thirds(values):
    high = values.astype(BF16)
    rest = values - high.astype(F32)
    middle = rest.astype(BF16)
    low = (rest - middle.astype(F32)).astype(BF16)
    return jnp.concatenate([high, middle, low], axis=0)


def iota(shape, dim):
    return lax.broadcasted_iota(jnp.int32, shape, dim)


def mixer_kernel(
    ring, chips, heads, blocks,
    x_hbm, b_hbm, c_hbm, ld_ref, dy_hbm,
    rounded_out, grads, dg_ref,
    vec, coef, ldp, runc, runr, scale, gain, scaled, pieces, states, states_held, dev, inc, out_state,
    inner, ptotal, bal, mate_in, far_in, back_in,
    load_sem,
    chain_send, chain_recv, mate_send, mate_recv, far_send, far_recv, back_send, back_recv,
):
    place = lax.axis_index("ctx")
    head = lax.axis_index("head")
    core = lax.rem(head, 2)
    mate = head + 1 - 2 * core
    chip = lax.div(head, 2)
    pairs = heads // 2
    width = heads * HEAD_DIM
    half = BLOCK // 2

    loads = [
        pltpu.make_async_copy(dy_hbm, vec.at[0], load_sem.at[0]),
        pltpu.make_async_copy(x_hbm, vec.at[1], load_sem.at[1]),
        pltpu.make_async_copy(c_hbm, coef.at[0], load_sem.at[2]),
        pltpu.make_async_copy(b_hbm, coef.at[1], load_sem.at[3]),
    ]
    for copy in loads:
        copy.start()

    barrier = pltpu.get_barrier_semaphore()
    pl.semaphore_signal(barrier, inc=1, device_id={"head": mate}, device_id_type=MESH)
    for hop in range(1, chips):
        pl.semaphore_signal(
            barrier, inc=1, device_id={"head": lax.rem(head + 2 * hop, 2 * chips)}, device_id_type=MESH
        )

    @pl.when(place > 0)
    def _():
        pl.semaphore_signal(barrier, inc=1, device_id={"ctx": place - 1}, device_id_type=MESH)

    @pl.when(place < ring - 1)
    def _():
        pl.semaphore_signal(barrier, inc=1, device_id={"ctx": place + 1}, device_id_type=MESH)

    slots = ldp.shape[0]
    ldp[...] = jnp.zeros_like(ldp)
    ldp[0:heads, :] = ld_ref[...]
    upper = (iota((BLOCK, BLOCK), 0) <= iota((BLOCK, BLOCK), 1)).astype(F32).astype(BF16)
    spread = (iota((slots, width), 0) == lax.div(iota((slots, width), 1), HEAD_DIM)).astype(F32)
    spread3 = jnp.concatenate([spread] * 3, axis=0).astype(BF16)
    gather = spread.astype(BF16)

    def joined(left3, right):
        three = mxu(left3, right, ((1,), (0,)))
        return three[0:slots] + three[slots : 2 * slots] + three[2 * slots :]

    for j in range(blocks):
        rows = slice(j * BLOCK, (j + 1) * BLOCK)
        run = joined(thirds(ldp[:, rows]), upper) * LOG2E
        runr[j] = run
        runc[j] = jnp.concatenate([run, jnp.zeros((LANES - slots, BLOCK), F32)], axis=0).T
        grow = mxu(thirds(jnp.exp2(run)), spread3, ((0,), (0,)))
        scale[0, rows, :] = grow
        scale[1, rows, :] = mxu(
            thirds(jnp.exp2(run[:, BLOCK - 1 :] - run)), spread3, ((0,), (0,))
        )
        gain[j] = jnp.broadcast_to(grow[BLOCK - 1 :, :], (8, width))

    for copy in loads:
        copy.wait()

    for j in range(blocks):
        for d in range(2):
            rows = slice(j * BLOCK, (j + 1) * BLOCK)
            row = (vec[d, rows, :].astype(F32) * scale[d, rows, :]).astype(BF16)
            scaled[d, rows, :] = row
            pieces[1 - d, j] = mxu(coef[d, rows, :], row, ((0,), (0,)))

    for p in range(pairs):
        lanes = slice(p * LANES, (p + 1) * LANES)
        product = gain[0, 0:1, lanes]
        forward = pieces[0, 0, :, lanes]
        backward = pieces[1, blocks - 1, :, lanes]
        for j in range(1, blocks):
            product = product * gain[j, 0:1, lanes]
            forward = gain[j, 0:1, lanes] * forward + pieces[0, j, :, lanes]
            k = blocks - 1 - j
            backward = gain[k, 0:1, lanes] * backward + pieces[1, k, :, lanes]
        dev[0, p] = forward
        dev[1, p] = backward
        gain[blocks + p, :, 0:LANES] = jnp.broadcast_to(product, (8, LANES))

    pl.semaphore_wait(barrier, chips + (place > 0).astype(jnp.int32) + (place < ring - 1).astype(jnp.int32))

    first = (2 * place > ring - 1).astype(jnp.int32)
    second = 1 - first

    def hops(d):
        return jnp.where(d == 0, place, ring - 1 - place)

    def chain_copy(d, p):
        target = jnp.where(d == 0, place + 1, place - 1)
        return pltpu.make_async_remote_copy(
            src_ref=out_state.at[d, p],
            dst_ref=inc.at[d, p],
            send_sem=chain_send.at[d, p],
            recv_sem=chain_recv.at[d, p],
            device_id={"ctx": jnp.clip(target, 0, ring - 1)},
            device_id_type=MESH,
        )

    def relay(d, p):
        chain_copy(d, p).wait_recv()

        @pl.when(hops(d) < ring - 1)
        def _():
            out_state[d, p] = gain[blocks + p, 0:1, 0:LANES] * inc[d, p] + dev[d, p]
            chain_copy(d, p).start()

    for d in range(2):

        @pl.when(hops(d) == 0)
        def _():
            @pl.loop(0, pairs)
            def _(p):
                inc[d, p] = jnp.zeros((STATE, LANES), F32)
                if ring > 1:
                    out_state[d, p] = dev[d, p]
                    chain_copy(d, p).start()

    def tick(unit):
        for d in (first, second):
            since = unit - HOP_UNITS * hops(d)
            p = jnp.maximum(since, 0) // CHUNK_UNITS

            @pl.when((hops(d) > 0) & (since >= 0) & (since == p * CHUNK_UNITS) & (p < pairs))
            def _():
                relay(d, p)

    last_unit = HOP_UNITS * (ring - 1) + CHUNK_UNITS * (pairs - 1) + 1

    low_lanes = iota((1, LANES), 1) < HEAD_DIM

    @pl.loop(0, blocks)
    def _(j):
        rows = pl.ds(pl.multiple_of(j * BLOCK, BLOCK), BLOCK)
        causal = iota((BLOCK, BLOCK), 0) >= iota((BLOCK, BLOCK), 1)
        scores = jnp.where(causal, mxu(coef[0, rows, :], coef[1, rows, :], ((1,), (1,))), 0.0)
        ptotal[0] = scores
        for p in range(pairs):
            lanes = slice(p * LANES, (p + 1) * LANES)
            x2 = vec[1, rows, lanes]
            dy2 = vec[0, rows, lanes]
            y2 = None
            for k in range(2):
                h = 2 * p + k
                mine = low_lanes if k == 0 else jnp.logical_not(low_lanes)
                xm = jnp.where(mine, x2, jnp.zeros_like(x2))
                dym = jnp.where(mine, dy2, jnp.zeros_like(dy2))
                decays = jnp.exp2(jnp.minimum(runc[j, :, h : h + 1] - runr[j, h : h + 1, :], 0.0))
                weights = (ptotal[0] * decays).astype(BF16)
                pair = mxu(dy2, xm, ((1,), (1,))) * decays
                if h == 0:
                    ptotal[1] = pair
                else:
                    ptotal[1] += pair
                y_add = mxu(weights, xm, ((1,), (0,)))
                dx_add = mxu(weights, dym, ((0,), (0,)))
                y2 = y_add if y2 is None else y2 + y_add
                dx2 = dx_add if k == 0 else dx2 + dx_add
            inner[0, rows, lanes] = y2
            inner[1, rows, lanes] = dx2
            tick(j * pairs + p)
        both = jnp.where(causal, ptotal[1], 0.0).astype(BF16)
        grads[0, rows, :] = mxu(both, coef[1, rows, :], ((1,), (0,)))
        grads[1, rows, :] = mxu(both, coef[0, rows, :], ((0,), (0,)))

    own_rows = core * half
    mate_rows = half - own_rows

    def piece_of(j, at):
        return pl.ds(pl.multiple_of(j * BLOCK + at, half), half)

    def mate_copy(d, j):
        return pltpu.make_async_remote_copy(
            src_ref=grads.at[d, piece_of(j, mate_rows), :],
            dst_ref=mate_in.at[d, j],
            send_sem=mate_send.at[d, j],
            recv_sem=mate_recv.at[d, j],
            device_id={"head": mate},
            device_id_type=MESH,
        )

    def far_copy(d, j, hop):
        return pltpu.make_async_remote_copy(
            src_ref=mate_in.at[d, j],
            dst_ref=far_in.at[d, j, chip],
            send_sem=far_send.at[d, j, hop],
            recv_sem=far_recv.at[d, j, chip],
            device_id={"head": lax.rem(head + 2 * hop, 2 * chips)},
            device_id_type=MESH,
        )

    def far_arrival(d, j, hop):
        source = lax.rem(chip + chips - hop, chips)
        return pltpu.make_async_remote_copy(
            src_ref=mate_in.at[d, j],
            dst_ref=far_in.at[d, j, source],
            send_sem=far_send.at[d, j, hop],
            recv_sem=far_recv.at[d, j, source],
            device_id={"head": lax.rem(head + 2 * hop, 2 * chips)},
            device_id_type=MESH,
        )

    def back_copy(d, j):
        return pltpu.make_async_remote_copy(
            src_ref=grads.at[d, piece_of(j, own_rows), :],
            dst_ref=back_in.at[d, j],
            send_sem=back_send.at[d, j],
            recv_sem=back_recv.at[d, j],
            device_id={"head": mate},
            device_id_type=MESH,
        )

    def local_sum(d, j):
        mate_copy(d, j).wait_recv()
        total = mate_in[d, j] + grads[d, piece_of(j, own_rows), :]
        mate_in[d, j] = total
        far_in[d, j, chip] = total
        for hop in range(1, chips):
            far_copy(d, j, hop).start()

    def far_sum(d, j):
        for hop in range(1, chips):
            far_arrival(d, j, hop).wait_recv()
        total = far_in[d, j, 0]
        for source in range(1, chips):
            total = total + far_in[d, j, source]
        grads[d, piece_of(j, own_rows), :] = total
        back_copy(d, j).start()

    def order(d, i):
        return jnp.where(d == 0, i, blocks - 1 - i)

    def outer_grads(d, start, ticking):
        states[d, blocks] = jnp.concatenate([inc[d, p] for p in range(pairs)], axis=1)

        @pl.loop(0, blocks)
        def _(i):
            j = order(d, i)
            rows = pl.ds(pl.multiple_of(j * BLOCK, BLOCK), BLOCK)
            now = states[d, blocks]
            states[d, j] = now
            states[d, blocks] = gain[j, 0:1, :] * now + pieces[d, j]
            held = now.astype(BF16)
            states_held[d, j] = held
            grads[d, rows, :] += mxu(scaled[d, rows, :], held, ((1,), (1,)))
            mate_copy(d, j).start()
            if ticking:
                tick(start + i)

            @pl.when(i > 0)
            def _():
                local_sum(d, order(d, i - 1))

        local_sum(d, order(d, blocks - 1))

    def outer_rows(d, start, ticking):
        @pl.loop(0, blocks)
        def _(i):
            j = order(d, i)
            rows = pl.ds(pl.multiple_of(j * BLOCK, BLOCK), BLOCK)
            held = states_held[d, j]
            full = inner[d, rows, :] + scale[d, rows, :] * mxu(coef[d, rows, :], held, ((1,), (0,)))
            rounded_out[d, rows, :] = full.astype(BF16)
            term = vec[d, rows, :].astype(F32) * full
            high = term.astype(BF16)
            low = (term - high.astype(F32)).astype(BF16)
            summed = mxu(gather, high, ((1,), (1,))) + mxu(gather, low, ((1,), (1,)))
            summed = jnp.where(d == 0, summed, -summed)
            if ticking:
                bal[j] = summed
                tick(start + i)
            else:
                bal[j] += summed

    units = blocks * pairs

    @pl.loop(units, jnp.maximum(units, HOP_UNITS * hops(first) + CHUNK_UNITS * (pairs - 1) + 1))
    def _(u):
        tick(u)

    start = jnp.maximum(units, HOP_UNITS * hops(first) + CHUNK_UNITS * (pairs - 1) + 1)
    outer_grads(first, start, True)
    outer_rows(first, start + blocks, True)
    start = start + 2 * blocks

    @pl.loop(start, jnp.maximum(start, last_unit))
    def _(u):
        tick(u)

    outer_grads(second, 0, False)

    @pl.loop(0, blocks)
    def _(i):
        far_sum(first, order(first, i))

    outer_rows(second, 0, False)

    for j in range(blocks):
        joint = jnp.sum(states[0, j + 1] * states[1, j], axis=0, keepdims=True)
        later = jnp.sum(spread * joint, axis=1, keepdims=True)
        lower = (iota((BLOCK, BLOCK), 0) >= iota((BLOCK, BLOCK), 1)).astype(F32).astype(BF16)
        suffix = joined(thirds(bal[j]), lower) + later
        dg_ref[:, j * BLOCK : (j + 1) * BLOCK] = suffix[0:heads, :]

    @pl.loop(0, blocks)
    def _(i):
        far_sum(second, order(second, i))

    @pl.loop(0, blocks)
    def _(j):
        for d in range(2):
            mate_copy(d, j).wait_send()
            back_copy(d, j).wait_recv()
            grads[d, piece_of(j, mate_rows), :] = back_in[d, j]

    @pl.loop(0, blocks)
    def _(j):
        for d in range(2):
            back_copy(d, j).wait_send()
            for hop in range(1, chips):
                far_copy(d, j, hop).wait_send()

    for d in range(2):

        @pl.when(hops(d) < ring - 1)
        def _():
            @pl.loop(0, pairs)
            def _(p):
                chain_copy(d, p).wait_send()


def store_kernel(rounded_out, grads, dg_in, y_hbm, dx_hbm, db_hbm, dc_hbm, dg_hbm, sem):
    copies = [
        pltpu.make_async_copy(rounded_out.at[0], y_hbm, sem.at[0]),
        pltpu.make_async_copy(rounded_out.at[1], dx_hbm, sem.at[1]),
        pltpu.make_async_copy(grads.at[1], db_hbm, sem.at[2]),
        pltpu.make_async_copy(grads.at[0], dc_hbm, sem.at[3]),
        pltpu.make_async_copy(dg_in, dg_hbm, sem.at[4]),
    ]
    for copy in copies:
        copy.start()
    for copy in copies:
        copy.wait()


def per_device(ring, chips, inputs, write_coeffs, read_coeffs, log_decay, out_grad):
    tokens = inputs.shape[0]
    real = log_decay.shape[1]
    heads = real + real % 2
    if heads > real:
        extra = ((0, 0), (0, (heads - real) * HEAD_DIM))
        inputs = jnp.pad(inputs, extra)
        out_grad = jnp.pad(out_grad, extra)
        log_decay = jnp.pad(log_decay, ((0, 0), (0, heads - real)))
    width = heads * HEAD_DIM
    blocks = tokens // BLOCK
    pairs = heads // 2
    half = BLOCK // 2
    slots = -(-heads // 16) * 16
    any_spec = pl.BlockSpec(memory_space=pl.ANY)
    hbm_spec = pl.BlockSpec(memory_space=pltpu.HBM)
    vmem_spec = pl.BlockSpec(memory_space=pltpu.VMEM)
    dma = pltpu.SemaphoreType.DMA
    held = pl.pallas_call(
        functools.partial(mixer_kernel, ring, chips, heads, blocks),
        out_shape=(
            pltpu.VMEM((2, tokens, width), BF16),
            pltpu.VMEM((2, tokens, STATE), F32),
            pltpu.VMEM((heads, tokens), F32),
        ),
        in_specs=[hbm_spec, hbm_spec, hbm_spec, vmem_spec, hbm_spec],
        out_specs=(vmem_spec, vmem_spec, vmem_spec),
        scratch_shapes=[
            pltpu.VMEM((2, tokens, width), BF16),
            pltpu.VMEM((2, tokens, STATE), BF16),
            pltpu.VMEM((slots, tokens), F32),
            pltpu.VMEM((blocks, BLOCK, LANES), F32),
            pltpu.VMEM((blocks, slots, BLOCK), F32),
            pltpu.VMEM((2, tokens, width), F32),
            pltpu.VMEM((blocks + pairs, 8, width), F32),
            pltpu.VMEM((2, tokens, width), BF16),
            pltpu.VMEM((2, blocks, STATE, width), F32),
            pltpu.VMEM((2, blocks + 1, STATE, width), F32),
            pltpu.VMEM((2, blocks, STATE, width), BF16),
            pltpu.VMEM((2, pairs, STATE, LANES), F32),
            pltpu.VMEM((2, pairs, STATE, LANES), F32),
            pltpu.VMEM((2, pairs, STATE, LANES), F32),
            pltpu.VMEM((2, tokens, width), F32),
            pltpu.VMEM((2, BLOCK, BLOCK), F32),
            pltpu.VMEM((blocks, slots, BLOCK), F32),
            pltpu.VMEM((2, blocks, half, STATE), F32),
            pltpu.VMEM((2, blocks, chips, half, STATE), F32),
            pltpu.VMEM((2, blocks, half, STATE), F32),
            dma((4,)),
            dma((2, pairs)),
            dma((2, pairs)),
            dma((2, blocks)),
            dma((2, blocks)),
            dma((2, blocks, chips)),
            dma((2, blocks, chips)),
            dma((2, blocks)),
            dma((2, blocks)),
        ],
        compiler_params=pltpu.CompilerParams(
            collective_id=0, has_side_effects=True, vmem_limit_bytes=36 * 1024 * 1024
        ),
    )(inputs, write_coeffs, read_coeffs, log_decay.T, out_grad)
    y, dx, db, dc, dg = pl.pallas_call(
        store_kernel,
        out_shape=(
            jax.ShapeDtypeStruct((tokens, width), BF16),
            jax.ShapeDtypeStruct((tokens, width), BF16),
            jax.ShapeDtypeStruct((tokens, STATE), F32),
            jax.ShapeDtypeStruct((tokens, STATE), F32),
            jax.ShapeDtypeStruct((heads, tokens), F32),
        ),
        in_specs=[vmem_spec] * 3,
        out_specs=(any_spec,) * 5,
        scratch_shapes=[dma((5,))],
        compiler_params=pltpu.CompilerParams(vmem_limit_bytes=8 * 1024 * 1024),
    )(*[pltpu.with_memory_space_constraint(piece, pltpu.VMEM) for piece in held])
    dg = dg.T
    if heads > real:
        y = y[:, : real * HEAD_DIM]
        dx = dx[:, : real * HEAD_DIM]
        dg = dg[:, :real]
    return (y, dx, db, dc, dg)


def solution(mesh):
    in_specs = (
        P(("grp", "ctx"), "head"),
        P(("grp", "ctx"), None),
        P(("grp", "ctx"), None),
        P(("grp", "ctx"), "head"),
        P(("grp", "ctx"), "head"),
    )
    out_specs = (
        P(("grp", "ctx"), "head"),
        P(("grp", "ctx"), "head"),
        P(("grp", "ctx"), None),
        P(("grp", "ctx"), None),
        P(("grp", "ctx"), "head"),
    )
    return jax.shard_map(
        functools.partial(per_device, mesh.shape["ctx"], mesh.shape["head"] // 2),
        mesh=mesh,
        in_specs=in_specs,
        out_specs=out_specs,
        check_vma=False,
    )
```

```python
import functools
import math

import jax
import jax.numpy as jnp
from jax import lax
from jax.experimental import pallas as pl
from jax.experimental.pallas import tpu as pltpu
from jax.sharding import PartitionSpec as P

HEAD_DIM = 64
STATE = 128
BLOCK = 256
LANES = 128
HOP_UNITS = 7
CHUNK_UNITS = 3
LOG2E = math.log2(math.e)
F32 = jnp.float32
BF16 = jnp.bfloat16
MESH = pl.DeviceIdType.MESH


def mxu(left, right, contract, precision=None):
    return lax.dot_general(
        left, right, (contract, ((), ())), preferred_element_type=F32, precision=precision
    )


def thirds(values):
    high = values.astype(BF16)
    rest = values - high.astype(F32)
    middle = rest.astype(BF16)
    low = (rest - middle.astype(F32)).astype(BF16)
    return jnp.concatenate([high, middle, low], axis=0)


def iota(shape, dim):
    return lax.broadcasted_iota(jnp.int32, shape, dim)


def mixer_kernel(
    ring, chips, heads, blocks,
    x_hbm, b_hbm, c_hbm, ld_ref, dy_hbm,
    rounded_out, grads, dg_ref,
    vec, coef, ldp, runc, runr, scale, gain, scaled, pieces, states, states_held, dev, inc, out_state,
    inner, ptotal, bal, mate_in, far_in, back_in,
    load_sem,
    chain_send, chain_recv, mate_send, mate_recv, far_send, far_recv, back_send, back_recv,
):
    place = lax.axis_index("ctx")
    head = lax.axis_index("head")
    core = lax.rem(head, 2)
    mate = head + 1 - 2 * core
    chip = lax.div(head, 2)
    pairs = heads // 2
    width = heads * HEAD_DIM
    half = BLOCK // 2

    loads = [
        pltpu.make_async_copy(dy_hbm, vec.at[0], load_sem.at[0]),
        pltpu.make_async_copy(x_hbm, vec.at[1], load_sem.at[1]),
        pltpu.make_async_copy(c_hbm, coef.at[0], load_sem.at[2]),
        pltpu.make_async_copy(b_hbm, coef.at[1], load_sem.at[3]),
    ]
    for copy in loads:
        copy.start()

    barrier = pltpu.get_barrier_semaphore()
    pl.semaphore_signal(barrier, inc=1, device_id={"head": mate}, device_id_type=MESH)
    for hop in range(1, chips):
        pl.semaphore_signal(
            barrier, inc=1, device_id={"head": lax.rem(head + 2 * hop, 2 * chips)}, device_id_type=MESH
        )

    @pl.when(place > 0)
    def _():
        pl.semaphore_signal(barrier, inc=1, device_id={"ctx": place - 1}, device_id_type=MESH)

    @pl.when(place < ring - 1)
    def _():
        pl.semaphore_signal(barrier, inc=1, device_id={"ctx": place + 1}, device_id_type=MESH)

    slots = ldp.shape[0]
    ldp[...] = jnp.zeros_like(ldp)
    ldp[0:heads, :] = ld_ref[...]
    upper = (iota((BLOCK, BLOCK), 0) <= iota((BLOCK, BLOCK), 1)).astype(F32).astype(BF16)
    spread = (iota((slots, width), 0) == lax.div(iota((slots, width), 1), HEAD_DIM)).astype(F32)
    spread3 = jnp.concatenate([spread] * 3, axis=0).astype(BF16)
    gather = spread.astype(BF16)

    def joined(left3, right):
        three = mxu(left3, right, ((1,), (0,)))
        return three[0:slots] + three[slots : 2 * slots] + three[2 * slots :]

    for j in range(blocks):
        rows = slice(j * BLOCK, (j + 1) * BLOCK)
        run = joined(thirds(ldp[:, rows]), upper) * LOG2E
        runr[j] = run
        runc[j] = jnp.concatenate([run, jnp.zeros((LANES - slots, BLOCK), F32)], axis=0).T
        grow = mxu(thirds(jnp.exp2(run)), spread3, ((0,), (0,)))
        scale[0, rows, :] = grow
        scale[1, rows, :] = mxu(
            thirds(jnp.exp2(run[:, BLOCK - 1 :] - run)), spread3, ((0,), (0,))
        )
        gain[j] = jnp.broadcast_to(grow[BLOCK - 1 :, :], (8, width))

    for copy in loads:
        copy.wait()

    for j in range(blocks):
        for d in range(2):
            rows = slice(j * BLOCK, (j + 1) * BLOCK)
            row = (vec[d, rows, :].astype(F32) * scale[d, rows, :]).astype(BF16)
            scaled[d, rows, :] = row
            pieces[1 - d, j] = mxu(coef[d, rows, :], row, ((0,), (0,)))

    for p in range(pairs):
        lanes = slice(p * LANES, (p + 1) * LANES)
        product = gain[0, 0:1, lanes]
        forward = pieces[0, 0, :, lanes]
        backward = pieces[1, blocks - 1, :, lanes]
        for j in range(1, blocks):
            product = product * gain[j, 0:1, lanes]
            forward = gain[j, 0:1, lanes] * forward + pieces[0, j, :, lanes]
            k = blocks - 1 - j
            backward = gain[k, 0:1, lanes] * backward + pieces[1, k, :, lanes]
        dev[0, p] = forward
        dev[1, p] = backward
        gain[blocks + p, :, 0:LANES] = jnp.broadcast_to(product, (8, LANES))

    pl.semaphore_wait(barrier, chips + (place > 0).astype(jnp.int32) + (place < ring - 1).astype(jnp.int32))

    first = (2 * place > ring - 1).astype(jnp.int32)
    second = 1 - first

    def hops(d):
        return jnp.where(d == 0, place, ring - 1 - place)

    def chain_copy(d, p):
        target = jnp.where(d == 0, place + 1, place - 1)
        return pltpu.make_async_remote_copy(
            src_ref=out_state.at[d, p],
            dst_ref=inc.at[d, p],
            send_sem=chain_send.at[d, p],
            recv_sem=chain_recv.at[d, p],
            device_id={"ctx": jnp.clip(target, 0, ring - 1)},
            device_id_type=MESH,
        )

    def relay(d, p):
        chain_copy(d, p).wait_recv()

        @pl.when(hops(d) < ring - 1)
        def _():
            out_state[d, p] = gain[blocks + p, 0:1, 0:LANES] * inc[d, p] + dev[d, p]
            chain_copy(d, p).start()

    for d in range(2):

        @pl.when(hops(d) == 0)
        def _():
            @pl.loop(0, pairs)
            def _(p):
                inc[d, p] = jnp.zeros((STATE, LANES), F32)
                if ring > 1:
                    out_state[d, p] = dev[d, p]
                    chain_copy(d, p).start()

    def tick(unit):
        for d in (first, second):
            since = unit - HOP_UNITS * hops(d)
            p = jnp.maximum(since, 0) // CHUNK_UNITS

            @pl.when((hops(d) > 0) & (since >= 0) & (since == p * CHUNK_UNITS) & (p < pairs))
            def _():
                relay(d, p)

    last_unit = HOP_UNITS * (ring - 1) + CHUNK_UNITS * (pairs - 1) + 1

    low_lanes = iota((1, LANES), 1) < HEAD_DIM

    @pl.loop(0, blocks)
    def _(j):
        rows = pl.ds(pl.multiple_of(j * BLOCK, BLOCK), BLOCK)
        causal = iota((BLOCK, BLOCK), 0) >= iota((BLOCK, BLOCK), 1)
        scores = jnp.where(causal, mxu(coef[0, rows, :], coef[1, rows, :], ((1,), (1,))), 0.0)
        ptotal[0] = scores
        for p in range(pairs):
            lanes = slice(p * LANES, (p + 1) * LANES)
            x2 = vec[1, rows, lanes]
            dy2 = vec[0, rows, lanes]
            y2 = None
            for k in range(2):
                h = 2 * p + k
                mine = low_lanes if k == 0 else jnp.logical_not(low_lanes)
                xm = jnp.where(mine, x2, jnp.zeros_like(x2))
                dym = jnp.where(mine, dy2, jnp.zeros_like(dy2))
                decays = jnp.exp2(jnp.minimum(runc[j, :, h : h + 1] - runr[j, h : h + 1, :], 0.0))
                weights = (ptotal[0] * decays).astype(BF16)
                pair = mxu(dy2, xm, ((1,), (1,))) * decays
                if h == 0:
                    ptotal[1] = pair
                else:
                    ptotal[1] += pair
                y_add = mxu(weights, xm, ((1,), (0,)))
                dx_add = mxu(weights, dym, ((0,), (0,)))
                y2 = y_add if y2 is None else y2 + y_add
                dx2 = dx_add if k == 0 else dx2 + dx_add
            inner[0, rows, lanes] = y2
            inner[1, rows, lanes] = dx2
            tick(j * pairs + p)
        both = jnp.where(causal, ptotal[1], 0.0).astype(BF16)
        grads[0, rows, :] = mxu(both, coef[1, rows, :], ((1,), (0,)))
        grads[1, rows, :] = mxu(both, coef[0, rows, :], ((0,), (0,)))

    own_rows = core * half
    mate_rows = half - own_rows

    def piece_of(j, at):
        return pl.ds(pl.multiple_of(j * BLOCK + at, half), half)

    def mate_copy(d, j):
        return pltpu.make_async_remote_copy(
            src_ref=grads.at[d, piece_of(j, mate_rows), :],
            dst_ref=mate_in.at[d, j],
            send_sem=mate_send.at[d, j],
            recv_sem=mate_recv.at[d, j],
            device_id={"head": mate},
            device_id_type=MESH,
        )

    def far_copy(d, j, hop):
        return pltpu.make_async_remote_copy(
            src_ref=mate_in.at[d, j],
            dst_ref=far_in.at[d, j, chip],
            send_sem=far_send.at[d, j, hop],
            recv_sem=far_recv.at[d, j, chip],
            device_id={"head": lax.rem(head + 2 * hop, 2 * chips)},
            device_id_type=MESH,
        )

    def far_arrival(d, j, hop):
        source = lax.rem(chip + chips - hop, chips)
        return pltpu.make_async_remote_copy(
            src_ref=mate_in.at[d, j],
            dst_ref=far_in.at[d, j, source],
            send_sem=far_send.at[d, j, hop],
            recv_sem=far_recv.at[d, j, source],
            device_id={"head": lax.rem(head + 2 * hop, 2 * chips)},
            device_id_type=MESH,
        )

    def back_copy(d, j):
        return pltpu.make_async_remote_copy(
            src_ref=grads.at[d, piece_of(j, own_rows), :],
            dst_ref=back_in.at[d, j],
            send_sem=back_send.at[d, j],
            recv_sem=back_recv.at[d, j],
            device_id={"head": mate},
            device_id_type=MESH,
        )

    def local_sum(d, j):
        mate_copy(d, j).wait_recv()
        total = mate_in[d, j] + grads[d, piece_of(j, own_rows), :]
        mate_in[d, j] = total
        far_in[d, j, chip] = total
        for hop in range(1, chips):
            far_copy(d, j, hop).start()

    def far_sum(d, j):
        for hop in range(1, chips):
            far_arrival(d, j, hop).wait_recv()
        total = far_in[d, j, 0]
        for source in range(1, chips):
            total = total + far_in[d, j, source]
        grads[d, piece_of(j, own_rows), :] = total
        back_copy(d, j).start()

    def order(d, i):
        return jnp.where(d == 0, i, blocks - 1 - i)

    def outer_grads(d, start, ticking):
        states[d, blocks] = jnp.concatenate([inc[d, p] for p in range(pairs)], axis=1)

        @pl.loop(0, blocks)
        def _(i):
            j = order(d, i)
            rows = pl.ds(pl.multiple_of(j * BLOCK, BLOCK), BLOCK)
            now = states[d, blocks]
            states[d, j] = now
            states[d, blocks] = gain[j, 0:1, :] * now + pieces[d, j]
            held = now.astype(BF16)
            states_held[d, j] = held
            grads[d, rows, :] += mxu(scaled[d, rows, :], held, ((1,), (1,)))
            mate_copy(d, j).start()
            if ticking:
                tick(start + i)

            @pl.when(i > 0)
            def _():
                local_sum(d, order(d, i - 1))

        local_sum(d, order(d, blocks - 1))

    def outer_rows(d, start, ticking):
        @pl.loop(0, blocks)
        def _(i):
            j = order(d, i)
            rows = pl.ds(pl.multiple_of(j * BLOCK, BLOCK), BLOCK)
            held = states_held[d, j]
            full = inner[d, rows, :] + scale[d, rows, :] * mxu(coef[d, rows, :], held, ((1,), (0,)))
            rounded_out[d, rows, :] = full.astype(BF16)
            term = vec[d, rows, :].astype(F32) * full
            high = term.astype(BF16)
            low = (term - high.astype(F32)).astype(BF16)
            summed = mxu(gather, high, ((1,), (1,))) + mxu(gather, low, ((1,), (1,)))
            summed = jnp.where(d == 0, summed, -summed)
            if ticking:
                bal[j] = summed
                tick(start + i)
            else:
                bal[j] += summed

    units = blocks * pairs

    @pl.loop(units, jnp.maximum(units, HOP_UNITS * hops(first) + CHUNK_UNITS * (pairs - 1) + 1))
    def _(u):
        tick(u)

    start = jnp.maximum(units, HOP_UNITS * hops(first) + CHUNK_UNITS * (pairs - 1) + 1)
    outer_grads(first, start, True)
    outer_rows(first, start + blocks, True)
    start = start + 2 * blocks

    @pl.loop(start, jnp.maximum(start, last_unit))
    def _(u):
        tick(u)

    outer_grads(second, 0, False)

    @pl.loop(0, blocks)
    def _(i):
        far_sum(first, order(first, i))

    outer_rows(second, 0, False)

    for j in range(blocks):
        joint = jnp.sum(states[0, j + 1] * states[1, j], axis=0, keepdims=True)
        later = jnp.sum(spread * joint, axis=1, keepdims=True)
        lower = (iota((BLOCK, BLOCK), 0) >= iota((BLOCK, BLOCK), 1)).astype(F32).astype(BF16)
        suffix = joined(thirds(bal[j]), lower) + later
        dg_ref[:, j * BLOCK : (j + 1) * BLOCK] = suffix[0:heads, :]

    @pl.loop(0, blocks)
    def _(i):
        far_sum(second, order(second, i))

    @pl.loop(0, blocks)
    def _(j):
        for d in range(2):
            mate_copy(d, j).wait_send()
            back_copy(d, j).wait_recv()
            grads[d, piece_of(j, mate_rows), :] = back_in[d, j]

    @pl.loop(0, blocks)
    def _(j):
        for d in range(2):
            back_copy(d, j).wait_send()
            for hop in range(1, chips):
                far_copy(d, j, hop).wait_send()

    for d in range(2):

        @pl.when(hops(d) < ring - 1)
        def _():
            @pl.loop(0, pairs)
            def _(p):
                chain_copy(d, p).wait_send()


def store_kernel(rounded_out, grads, dg_in, y_hbm, dx_hbm, db_hbm, dc_hbm, dg_hbm, sem):
    copies = [
        pltpu.make_async_copy(rounded_out.at[0], y_hbm, sem.at[0]),
        pltpu.make_async_copy(rounded_out.at[1], dx_hbm, sem.at[1]),
        pltpu.make_async_copy(grads.at[1], db_hbm, sem.at[2]),
        pltpu.make_async_copy(grads.at[0], dc_hbm, sem.at[3]),
        pltpu.make_async_copy(dg_in, dg_hbm, sem.at[4]),
    ]
    for copy in copies:
        copy.start()
    for copy in copies:
        copy.wait()


def hbm(array):
    return pltpu.with_memory_space_constraint(array, pltpu.HBM)


def per_device(ring, chips, inputs, write_coeffs, read_coeffs, log_decay, out_grad):
    tokens = inputs.shape[0]
    real = log_decay.shape[1]
    heads = real + real % 2
    if heads > real:
        extra = ((0, 0), (0, (heads - real) * HEAD_DIM))
        inputs = jnp.pad(inputs, extra)
        out_grad = jnp.pad(out_grad, extra)
        log_decay = jnp.pad(log_decay, ((0, 0), (0, heads - real)))
    width = heads * HEAD_DIM
    blocks = tokens // BLOCK
    pairs = heads // 2
    half = BLOCK // 2
    slots = -(-heads // 16) * 16
    any_spec = pl.BlockSpec(memory_space=pl.ANY)
    hbm_spec = pl.BlockSpec(memory_space=pltpu.HBM)
    vmem_spec = pl.BlockSpec(memory_space=pltpu.VMEM)
    dma = pltpu.SemaphoreType.DMA
    held = pl.pallas_call(
        functools.partial(mixer_kernel, ring, chips, heads, blocks),
        out_shape=(
            pltpu.VMEM((2, tokens, width), BF16),
            pltpu.VMEM((2, tokens, STATE), F32),
            pltpu.VMEM((heads, tokens), F32),
        ),
        in_specs=[hbm_spec, hbm_spec, hbm_spec, vmem_spec, hbm_spec],
        out_specs=(vmem_spec, vmem_spec, vmem_spec),
        scratch_shapes=[
            pltpu.VMEM((2, tokens, width), BF16),
            pltpu.VMEM((2, tokens, STATE), BF16),
            pltpu.VMEM((slots, tokens), F32),
            pltpu.VMEM((blocks, BLOCK, LANES), F32),
            pltpu.VMEM((blocks, slots, BLOCK), F32),
            pltpu.VMEM((2, tokens, width), F32),
            pltpu.VMEM((blocks + pairs, 8, width), F32),
            pltpu.VMEM((2, tokens, width), BF16),
            pltpu.VMEM((2, blocks, STATE, width), F32),
            pltpu.VMEM((2, blocks + 1, STATE, width), F32),
            pltpu.VMEM((2, blocks, STATE, width), BF16),
            pltpu.VMEM((2, pairs, STATE, LANES), F32),
            pltpu.VMEM((2, pairs, STATE, LANES), F32),
            pltpu.VMEM((2, pairs, STATE, LANES), F32),
            pltpu.VMEM((2, tokens, width), F32),
            pltpu.VMEM((2, BLOCK, BLOCK), F32),
            pltpu.VMEM((blocks, slots, BLOCK), F32),
            pltpu.VMEM((2, blocks, half, STATE), F32),
            pltpu.VMEM((2, blocks, chips, half, STATE), F32),
            pltpu.VMEM((2, blocks, half, STATE), F32),
            dma((4,)),
            dma((2, pairs)),
            dma((2, pairs)),
            dma((2, blocks)),
            dma((2, blocks)),
            dma((2, blocks, chips)),
            dma((2, blocks, chips)),
            dma((2, blocks)),
            dma((2, blocks)),
        ],
        compiler_params=pltpu.CompilerParams(
            collective_id=0, has_side_effects=True, vmem_limit_bytes=36 * 1024 * 1024
        ),
    )(hbm(inputs), hbm(write_coeffs), hbm(read_coeffs), log_decay.T, hbm(out_grad))
    y, dx, db, dc, dg = pl.pallas_call(
        store_kernel,
        out_shape=(
            jax.ShapeDtypeStruct((tokens, width), BF16),
            jax.ShapeDtypeStruct((tokens, width), BF16),
            jax.ShapeDtypeStruct((tokens, STATE), F32),
            jax.ShapeDtypeStruct((tokens, STATE), F32),
            jax.ShapeDtypeStruct((heads, tokens), F32),
        ),
        in_specs=[vmem_spec] * 3,
        out_specs=(any_spec,) * 5,
        scratch_shapes=[dma((5,))],
        compiler_params=pltpu.CompilerParams(vmem_limit_bytes=8 * 1024 * 1024),
    )(*[pltpu.with_memory_space_constraint(piece, pltpu.VMEM) for piece in held])
    dg = dg.T
    if heads > real:
        y = y[:, : real * HEAD_DIM]
        dx = dx[:, : real * HEAD_DIM]
        dg = dg[:, :real]
    return (y, dx, db, dc, dg)


def solution(mesh):
    in_specs = (
        P(("grp", "ctx"), "head"),
        P(("grp", "ctx"), None),
        P(("grp", "ctx"), None),
        P(("grp", "ctx"), "head"),
        P(("grp", "ctx"), "head"),
    )
    out_specs = (
        P(("grp", "ctx"), "head"),
        P(("grp", "ctx"), "head"),
        P(("grp", "ctx"), None),
        P(("grp", "ctx"), None),
        P(("grp", "ctx"), "head"),
    )
    return jax.shard_map(
        functools.partial(per_device, mesh.shape["ctx"], mesh.shape["head"] // 2),
        mesh=mesh,
        in_specs=in_specs,
        out_specs=out_specs,
        check_vma=False,
    )
```
